128 devices in a mesh: seq: 8 (over y, z_lo), chan: 16 (over z_hi, x, core).
Axes of the slice: x: 4, y: 4, z: 4 (z_hi: 2, z_lo: 2; z = z_hi * 2 + z_lo), core: 2. Of those that a mesh axis runs over, the one named last changes fastest.
Arguments:
- conv_input: bfloat16 [8192, 4096], P('seq', 'chan'), may hold values from -0.0078125 to 0.0078125
- grad_out: bfloat16 [8192, 4096], P(('seq', 'chan')), may hold values from -6 to 6
- out_weight: bfloat16 [4096, 4096], P('chan'), may hold values from -0.09375 to 0.09375
- filters: bfloat16 [128, 8192], P('chan'), may hold values from -0.0625 to 0.0625
Outputs:
- grad_input: bfloat16 [8192, 4096], P('seq', 'chan')
- grad_filters: float32 [128, 8192], P('chan', 'seq')
The draws below stay inside these ranges and needn't reach their ends.
All inputs are finite; a program needn't handle non-finite values.
Results may differ from the reference program's by a relative error of at most 0.0051.
Values may be sent and summed in bfloat16 or wider, within the bound.
No kernel may reach another device: no remote copies, remote signals or barrier semaphores. Data moves between devices by JAX's collectives and lax.ppermute only.
A program may use at most 512 MiB of HBM per device.

```python
import jax
import jax.numpy as jnp
from jax import lax

GROUPS = 128
GSIZE = 32
D = 4096
LAG = 8192
TOKENS = 8192


def steps_of(own_key, extent, shards, low, top_value):
    gain = 1.0
    for axis_at, blocks in shards:
        draws = jax.random.uniform(jax.random.fold_in(jax.random.fold_in(own_key, 6), axis_at), (blocks,), jnp.float32, low / len(shards), top_value / len(shards))
        gain = gain * jnp.repeat(jnp.exp(draws), extent[axis_at] // blocks).reshape((-1,) + (1,) * (len(extent) - 1 - axis_at))
    return gain


def scatter_about(own_key, extent, scale, most, split=(), kind=jnp.bfloat16):
    values = jax.random.normal(own_key, extent, jnp.float32) * scale
    if len(split) > 0:
        values = steps_of(own_key, extent, split, -0.22, 0.18) * values
    return jnp.clip(values, min=-most, max=most).astype(kind)


def setup_inputs(seed: int = 0) -> dict:
    arg_keys = jax.random.split(jax.random.key(seed), 5)
    return {
        "conv_input": scatter_about(arg_keys[0], (TOKENS, D), 0.0014, 0.0078125, ((0, 8), (1, 16))),
        "grad_out": scatter_about(arg_keys[1], (TOKENS, D), 1.0, 6.0, ((0, 128),)),
        "out_weight": scatter_about(arg_keys[2], (D, D), D ** -0.5, 0.09375, ((0, 16),)),
        "filters": scatter_about(arg_keys[3], (GROUPS, LAG), LAG ** -0.5, 0.0625, ((0, 16),)),
    }


def reference(conv_input, grad_out, out_weight, filters):
    grad_mid = jnp.dot(grad_out, out_weight.T, preferred_element_type=jnp.float32).astype(jnp.bfloat16)
    grad_mid = lax.optimization_barrier(grad_mid).astype(jnp.float32)
    inputs = conv_input.astype(jnp.float32)
    length = TOKENS + LAG
    grad_groups = grad_mid.reshape(TOKENS, GROUPS, GSIZE).transpose(1, 0, 2)
    input_groups = inputs.reshape(TOKENS, GROUPS, GSIZE).transpose(1, 0, 2)

    def per_group(items):
        grad_group, input_group, filter_group = items
        spec_grad = jnp.fft.rfft(grad_group, n=length, axis=0)
        spec_filter = jnp.fft.rfft(filter_group, n=length)
        spec_input = jnp.fft.rfft(input_group, n=length, axis=0)
        through = jnp.fft.irfft(spec_grad * jnp.conj(spec_filter)[:, None], n=length, axis=0)[:TOKENS]
        lagged = jnp.fft.irfft(jnp.sum(spec_grad * jnp.conj(spec_input), axis=1), n=length)[:LAG]
        return through, lagged

    through, lagged = lax.map(per_group, (grad_groups, input_groups, filters.astype(jnp.float32)))
    grad_input = through.transpose(1, 0, 2).reshape(TOKENS, D).astype(jnp.bfloat16)
    return grad_input, lagged.astype(jnp.float32)
```

```python
import functools

import jax
import jax.numpy as jnp
from jax import lax
from jax.experimental import pallas as pl
from jax.experimental.pallas import tpu as pltpu
from jax.sharding import Mesh
from jax.sharding import PartitionSpec as P

F32 = jnp.float32
BF16 = jnp.bfloat16

TILE = 128
BLK = 256
PART = 16
TAIL = 8
VMEM_MIB = 24
X_UP = [(i, (i + 1) % 4) for i in range(4)]
X_DOWN = [(i, (i - 1) % 4) for i in range(4)]
Z_NEAR = [(i, 3 - i) for i in range(4)]
SWAP = [(0, 1), (1, 0)]


def mm(a, b, dims=(((1,), (0,)), ((), ()))):
    return lax.dot_general(a, b, dims, preferred_element_type=F32)


def iota(shape, axis):
    return lax.broadcasted_iota(jnp.int32, shape, axis)


def params():
    return pltpu.CompilerParams(vmem_limit_bytes=VMEM_MIB * 2**20)


def cost(flops, moved):
    return pl.CostEstimate(flops=flops, bytes_accessed=moved, transcendentals=0)


def prep_body(x_ref, o_ref, *, groups, width):
    blocks = x_ref.shape[0] // BLK
    chans = x_ref.shape[1]
    flip = (iota((BLK, BLK), 0) + iota((BLK, BLK), 1) == BLK - 1).astype(BF16)
    turned = [
        mm(flip, x_ref[a * BLK : (a + 1) * BLK, :]).astype(BF16) for a in range(blocks)
    ]
    row = iota((chans, TILE), 0)
    col = iota((chans, TILE), 1)
    for g in range(groups):
        total = jnp.zeros((BLK, TILE), F32)
        for a in range(blocks):
            pick = (row - g * width == col - a * width) & (col // width == a)
            total = total + mm(turned[a], pick.astype(BF16))
        o_ref[g] = total.astype(BF16)


def prep_input(x, groups, width):
    return pl.pallas_call(
        functools.partial(prep_body, groups=groups, width=width),
        out_shape=jax.ShapeDtypeStruct((groups, BLK, TILE), BF16),
        name="prep_input",
        compiler_params=params(),
        cost_estimate=cost(2 * 10**9, 4 * x.size),
    )(x)


def tiles_body(f_ref, x_ref, o_ref, y_ref):
    for s in range(x_ref.shape[0]):
        y_ref[:, s * TILE : (s + 1) * TILE] = x_ref[s]
    count = f_ref.shape[0]
    flip = (iota((TILE, TILE), 0) + iota((TILE, TILE), 1) == TILE - 1).astype(BF16)
    turned = mm(f_ref[...], flip)
    o_ref[0] = jnp.zeros((TILE, TILE), BF16)
    zero = jnp.zeros((1, TILE), F32)
    for k in range(count):
        before = turned[k - 1 : k] if k else zero
        line = jnp.concatenate([before, turned[k : k + 1]], axis=1)
        spread = jnp.broadcast_to(line, (TILE, 2 * TILE))
        turn = pltpu.roll(spread, 1, 1, stride=1, stride_axis=0)
        o_ref[k + 1] = turn[:, :TILE].astype(BF16)


def toeplitz_tiles(f, x):
    count = f.shape[0]
    return pl.pallas_call(
        tiles_body,
        out_shape=(
            jax.ShapeDtypeStruct((count + 1, TILE, TILE), BF16),
            jax.ShapeDtypeStruct((BLK, x.shape[0] * TILE), BF16),
        ),
        name="toeplitz_tiles",
        compiler_params=params(),
        cost_estimate=cost(2 * 10**9, 2 * count * TILE * TILE),
    )(f, x)


def project_body(s_ref, own_ref, other_ref, *refs, shifts):
    blocks, o_ref, rows, acc = refs[:-3], refs[-3], refs[-2], refs[-1]
    k = pl.program_id(0)
    x = s_ref[0]
    core = s_ref[1]
    chans = own_ref.shape[0]
    size = rows.shape[0] // 4
    for ref, (shift, at) in zip(blocks, shifts):
        spot = lax.rem(x + shift, 4) * size + at
        rows[pl.ds(pl.multiple_of(spot, 32), ref.shape[0]), :] = ref[...]

    @pl.when(k == 0)
    def _():
        acc[...] = jnp.zeros_like(acc)

    dims = (((1,), (1,)), ((), ()))
    acc[:chans, :] += mm(own_ref[...], rows[...], dims)
    acc[chans:, :] += mm(other_ref[...], rows[...], dims)

    @pl.when(k == pl.num_programs(0) - 1)
    def _():
        at = pl.multiple_of(core * chans, chans)
        o_ref[pl.ds(at, chans), :] = acc[:chans, :].astype(BF16)
        at = pl.multiple_of((1 - core) * chans, chans)
        o_ref[pl.ds(at, chans), :] = acc[chans:, :].astype(BF16)


def project(spots, own, other, blocks, shifts, steps=4):
    chans, depth = own.shape
    step = depth // steps
    rows = sum(b.shape[0] for b in blocks)
    return pl.pallas_call(
        functools.partial(project_body, shifts=shifts),
        out_shape=jax.ShapeDtypeStruct((2 * chans, rows), BF16),
        grid_spec=pltpu.PrefetchScalarGridSpec(
            num_scalar_prefetch=1,
            grid=(steps,),
            in_specs=[pl.BlockSpec((chans, step), lambda k, s: (0, k))] * 2
            + [pl.BlockSpec((b.shape[0], step), lambda k, s: (0, k)) for b in blocks],
            out_specs=pl.BlockSpec((2 * chans, rows), lambda k, s: (0, 0)),
            scratch_shapes=[
                pltpu.VMEM((rows, step), BF16),
                pltpu.VMEM((2 * chans, rows), F32),
            ],
        ),
        name="project",
        compiler_params=params(),
        cost_estimate=cost(4 * chans * rows * depth, 2 * depth * (2 * chans + rows)),
    )(spots, own, other, *blocks)


def conv_body(s_ref, g0_ref, g1_ref, x_ref, t_ref, o_ref, gb, acc, corr):
    zhi = s_ref[0]
    width = g0_ref.shape[1]
    senders = g0_ref.shape[0] // 2
    nb = 4 * senders
    top = nb * width
    lane = iota((width, TILE), 1)
    gb[top:, :] = jnp.zeros((gb.shape[0] - top, BLK), BF16)
    for half, g_ref in enumerate((g0_ref, g1_ref)):
        for s in range(senders):
            owner = s ^ half
            zz = 1 - zhi if half else zhi
            for xh in range(2):
                lo = xh * TILE
                a = g_ref[s, :, lo : lo + TILE].astype(F32)
                b = g_ref[senders + s, :, lo : lo + TILE].astype(F32)
                left = jnp.where(lane < 64, a, pltpu.roll(b, 64, 1))
                right = jnp.where(lane < 64, pltpu.roll(a, 64, 1), b)
                spot = (owner * 4 + zz * 2 + xh) * width
                at = pl.ds(pl.multiple_of(spot, width), width)
                gb[at, :TILE] = left.astype(BF16)
                gb[at, TILE:] = right.astype(BF16)

    def put(k, value, fresh=False):
        for part in range(TILE // PART):
            piece = value[part * PART : (part + 1) * PART, :]
            at = slice(k * PART, (k + 1) * PART)
            if fresh:
                corr[part, at, :] = piece
            else:
                corr[part, at, :] += piece

    for d in range(nb):
        span = -(-(nb - d) * width // BLK) * BLK
        moved = gb[d * width : d * width + span, :]
        mid = t_ref[2 * d + 1]
        up = t_ref[2 * d + 2]
        down = t_ref[2 * d]
        tile = jnp.concatenate(
            [
                jnp.concatenate([mid, down], axis=1),
                jnp.concatenate([up, mid], axis=1),
            ],
            axis=0,
        )
        if d == 0:
            acc[...] = mm(moved, tile)
        else:
            acc[:span, :] += mm(moved, tile)
        prod = mm(x_ref[:, :span], moved)
        put(2 * d, prod[:TILE, :TILE], fresh=d == 0)
        put(2 * d + 1, prod[:TILE, TILE:] + prod[TILE:, :TILE], fresh=True)
        put(2 * d + 2, prod[TILE:, TILE:], fresh=True)

    for s in range(senders):
        for k in range(4):
            a = s * 4 + k
            o_ref[s, :width, k * BLK : (k + 1) * BLK] = acc[
                a * width : (a + 1) * width, :
            ].astype(BF16)

    lane = iota((PART, TILE), 1)
    turned = lane <= iota((PART, TILE), 0)
    spill = jnp.zeros((PART, TILE), F32)
    carry = jnp.zeros((1, TILE), F32)
    lines = []
    for k in range(2 * nb + 2):
        total = spill
        if k <= 2 * nb:
            low = corr[0, k * PART : (k + 1) * PART, :]
            spill = jnp.zeros((PART, TILE), F32)
            for part in range(1, TILE // PART):
                by = part * PART
                move = pltpu.roll(corr[part, k * PART : (k + 1) * PART, :], by, 1)
                low = low + jnp.where(lane >= by, move, 0.0)
                spill = spill + jnp.where(lane < by, move, 0.0)
            total = total + low
        move = pltpu.roll(total, 1, 1, stride=1, stride_axis=0)
        line = jnp.sum(jnp.where(turned, 0.0, move), axis=0, keepdims=True)
        if k >= 2:
            lines.append(line + carry)
        carry = jnp.sum(jnp.where(turned, move, 0.0), axis=0, keepdims=True)

    for s in range(senders):
        rest = jnp.concatenate(lines[s * TAIL : (s + 1) * TAIL], axis=0)
        for part in range(3):
            piece = rest.astype(BF16)
            o_ref[s, width:, part * TILE : (part + 1) * TILE] = piece
            rest = rest - piece.astype(F32)
        o_ref[s, width:, 3 * TILE :] = jnp.zeros((TAIL, o_ref.shape[2] - 3 * TILE), BF16)


def convolve(spot, g0, g1, xt, tiles):
    senders = g0.shape[0] // 2
    width = g0.shape[1]
    nb = 4 * senders
    top = nb * width
    return pl.pallas_call(
        conv_body,
        out_shape=jax.ShapeDtypeStruct((senders, width + TAIL, 4 * BLK), BF16),
        in_specs=[pl.BlockSpec(memory_space=pltpu.SMEM)]
        + [pl.BlockSpec(memory_space=pltpu.VMEM)] * 4,
        scratch_shapes=[
            pltpu.VMEM((top + BLK, BLK), BF16),
            pltpu.VMEM((top, BLK), F32),
            pltpu.VMEM((TILE // PART, (2 * nb + 1) * PART, TILE), F32),
        ],
        name="convolve",
        compiler_params=params(),
        cost_estimate=cost(6 * 10**9, 4 * 10**6),
    )(spot, g0, g1, xt, tiles)


def finish_body(m_ref, o_ref, f_ref):
    groups, rows, _ = m_ref.shape
    width = rows - TAIL
    for g in range(groups // 4):
        four = [m_ref[4 * g + i, :width, :].astype(F32) for i in range(4)]
        flat = jnp.concatenate(four, axis=0)
        o_ref[:, g * TILE : (g + 1) * TILE] = flat.T.astype(BF16)
    for g in range(groups):
        rest = m_ref[g, width:, : 3 * TILE].astype(F32)
        total = rest[:, :TILE] + rest[:, TILE : 2 * TILE] + rest[:, 2 * TILE :]
        for j in range(TAIL):
            f_ref[g : g + 1, j * TILE : (j + 1) * TILE] = total[j : j + 1, :]


def finish(major):
    groups, rows, span = major.shape
    return pl.pallas_call(
        finish_body,
        out_shape=(
            jax.ShapeDtypeStruct((span, groups * (rows - TAIL)), BF16),
            jax.ShapeDtypeStruct((groups, TAIL * TILE), F32),
        ),
        name="finish",
        compiler_params=params(),
        cost_estimate=cost(10**6, 4 * major.size),
    )(major)


def on_device(conv_input, grad_out, out_weight, filters):
    groups = filters.shape[0]
    width = conv_input.shape[1] // groups
    seq = ("y", "zlo")
    near = ("zlo", "zhi")
    x = lax.axis_index("x").astype(jnp.int32)
    core = lax.axis_index("core").astype(jnp.int32)
    zhi = lax.axis_index("zhi").astype(jnp.int32)
    half = grad_out.shape[0] // 2
    before = lax.ppermute(grad_out, "x", X_UP)
    after = lax.ppermute(grad_out, "x", X_DOWN)
    other_weight = lax.ppermute(out_weight, "core", SWAP)
    near_own = lax.ppermute(grad_out, near, Z_NEAR)
    turned = prep_input(conv_input, groups, width)
    turned = lax.all_to_all(turned, seq, 0, 0, tiled=True)
    far_a = lax.ppermute(before[:half], "x", X_UP)
    far_b = lax.ppermute(after[half:], "x", X_DOWN)
    near_before = lax.ppermute(near_own, "x", X_UP)
    near_after = lax.ppermute(near_own, "x", X_DOWN)
    near_far_a = lax.ppermute(far_a, near, Z_NEAR)
    near_far_b = lax.ppermute(far_b, near, Z_NEAR)
    tap = lax.dynamic_index_in_dim(filters, lax.axis_index(seq), 0, False)
    tiles, xt = toeplitz_tiles(tap.reshape(-1, TILE), turned)
    spots = jnp.stack([x, core])
    shifts = [(0, 0), (3, 0), (1, 0), (2, 0), (2, half)]
    everyone = ("core",) + seq
    g0 = project(
        spots, out_weight, other_weight,
        [grad_out, before, after, far_a, far_b], shifts,
    )
    g0 = lax.all_to_all(g0.reshape(2 * groups, width, -1), everyone, 0, 0, tiled=True)
    g1 = project(
        spots, out_weight, other_weight,
        [near_own, near_before, near_after, near_far_a, near_far_b], shifts,
    )
    g1 = lax.all_to_all(g1.reshape(2 * groups, width, -1), everyone, 0, 0, tiled=True)
    major = convolve(zhi.reshape(1), g0, g1, xt, tiles)
    major = lax.all_to_all(major, seq, 0, 0, tiled=True)
    return finish(major)


def solution(mesh):
    fine = Mesh(
        mesh.devices.reshape(4, 2, 2, 4, 2),
        ("y", "zlo", "zhi", "x", "core"),
        axis_types=(jax.sharding.AxisType.Auto,) * 5,
    )
    seq = ("y", "zlo")
    chan = ("zhi", "x", "core")
    in_specs = (P(seq, chan), P(seq + chan, None), P(chan, None), P(chan, None))
    out_specs = (P(seq, chan), P(chan, seq))
    return jax.shard_map(
        on_device, mesh=fine, in_specs=in_specs, out_specs=out_specs, check_vma=False
    )
```

```python
import functools

import jax
import jax.numpy as jnp
from jax import lax
from jax.experimental import pallas as pl
from jax.experimental.pallas import tpu as pltpu
from jax.sharding import Mesh
from jax.sharding import PartitionSpec as P

F32 = jnp.float32
BF16 = jnp.bfloat16

TILE = 128
BLK = 256
PART = 16
TAIL = 8
STEP = 1024
VMEM_MIB = 24
X_UP = [(i, (i + 1) % 4) for i in range(4)]
X_DOWN = [(i, (i - 1) % 4) for i in range(4)]
Z_NEAR = [(i, 3 - i) for i in range(4)]
SWAP = [(0, 1), (1, 0)]


def mm(a, b, dims=(((1,), (0,)), ((), ()))):
    return lax.dot_general(a, b, dims, preferred_element_type=F32)


def iota(shape, axis):
    return lax.broadcasted_iota(jnp.int32, shape, axis)


def params():
    return pltpu.CompilerParams(vmem_limit_bytes=VMEM_MIB * 2**20)


def cost(flops, moved):
    return pl.CostEstimate(flops=flops, bytes_accessed=moved, transcendentals=0)


def prep_body(x_ref, o_ref, *, groups, width):
    blocks = x_ref.shape[0] // BLK
    chans = x_ref.shape[1]
    flip = (iota((BLK, BLK), 0) + iota((BLK, BLK), 1) == BLK - 1).astype(BF16)
    turned = [
        mm(flip, x_ref[a * BLK : (a + 1) * BLK, :]).astype(BF16) for a in range(blocks)
    ]
    row = iota((chans, TILE), 0)
    col = iota((chans, TILE), 1)
    for g in range(groups):
        total = jnp.zeros((BLK, TILE), F32)
        for a in range(blocks):
            pick = (row - g * width == col - a * width) & (col // width == a)
            total = total + mm(turned[a], pick.astype(BF16))
        o_ref[g] = total.astype(BF16)


def prep_input(x, groups, width):
    return pl.pallas_call(
        functools.partial(prep_body, groups=groups, width=width),
        out_shape=jax.ShapeDtypeStruct((groups, BLK, TILE), BF16),
        name="prep_input",
        compiler_params=params(),
        cost_estimate=cost(2 * 10**9, 4 * x.size),
    )(x)


def project_body(s_ref, own_ref, other_ref, *refs, shifts, join):
    count = len(shifts)
    blocks, o_ref = refs[:count], refs[count + join]
    weight, rows, acc, sem = refs[count + join + 1 :]
    x = s_ref[0]
    core = s_ref[1]
    chans, depth = own_ref.shape
    size = rows.shape[0] // 4
    moves = [(own_ref, weight, 0), (other_ref, weight, chans)]
    for ref, (shift, at) in zip(blocks, shifts):
        spot = lax.rem(x + shift, 4) * size + at
        moves.append((ref, rows, pl.multiple_of(spot, 32)))
    copies = []
    for k in range(depth // STEP):
        span = pl.ds(k * STEP, STEP)
        for i, (ref, held, spot) in enumerate(moves):
            copy = pltpu.make_async_copy(
                ref.at[:, span], held.at[pl.ds(spot, ref.shape[0]), span], sem.at[k, i]
            )
            copy.start()
            copies.append(copy)
    width = rows.shape[0]
    if join:
        o_ref[:, :width] = refs[count][...]
    dims = (((1,), (1,)), ((), ()))
    for k in range(depth // STEP):
        for copy in copies[k * len(moves) : (k + 1) * len(moves)]:
            copy.wait()
        at = slice(k * STEP, (k + 1) * STEP)
        for half in range(2):
            spot = slice(half * chans, (half + 1) * chans)
            value = mm(weight[spot, at], rows[:, at], dims)
            if k:
                acc[spot, :] += value
            else:
                acc[spot, :] = value
    to = slice(join * width, (join + 1) * width)
    at = pl.multiple_of(core * chans, chans)
    o_ref[pl.ds(at, chans), to] = acc[:chans, :].astype(BF16)
    at = pl.multiple_of((1 - core) * chans, chans)
    o_ref[pl.ds(at, chans), to] = acc[chans:, :].astype(BF16)


def project(spots, own, other, blocks, shifts, first=None):
    chans, depth = own.shape
    rows = sum(b.shape[0] for b in blocks)
    extra = [] if first is None else [first]
    join = len(extra)
    return pl.pallas_call(
        functools.partial(project_body, shifts=shifts, join=join),
        out_shape=jax.ShapeDtypeStruct((2 * chans, (1 + join) * rows), BF16),
        in_specs=[pl.BlockSpec(memory_space=pltpu.SMEM)]
        + [pl.BlockSpec(memory_space=pl.ANY)] * (2 + len(blocks))
        + [pl.BlockSpec(memory_space=pltpu.VMEM)] * join,
        scratch_shapes=[
            pltpu.VMEM((2 * chans, depth), BF16),
            pltpu.VMEM((rows, depth), BF16),
            pltpu.VMEM((2 * chans, rows), F32),
            pltpu.SemaphoreType.DMA((depth // STEP, 2 + len(blocks))),
        ],
        name="project",
        compiler_params=params(),
        cost_estimate=cost(4 * chans * rows * depth, 2 * depth * (2 * chans + rows)),
    )(spots, own, other, *blocks, *extra)


def conv_body(s_ref, g_ref, x_ref, f_ref, o_ref, gb, acc, corr, t_ref):
    zhi = s_ref[0]
    width = g_ref.shape[1]
    senders = g_ref.shape[0] // 2
    nb = 4 * senders
    top = nb * width
    lane = iota((width, TILE), 1)
    gb[top:, :] = jnp.zeros((gb.shape[0] - top, BLK), BF16)
    for half in range(2):
        for s in range(senders):
            owner = s ^ half
            zz = 1 - zhi if half else zhi
            for xh in range(2):
                lo = (half * 2 + xh) * TILE
                a = g_ref[s, :, lo : lo + TILE].astype(F32)
                b = g_ref[senders + s, :, lo : lo + TILE].astype(F32)
                left = jnp.where(lane < 64, a, pltpu.roll(b, 64, 1))
                right = jnp.where(lane < 64, pltpu.roll(a, 64, 1), b)
                spot = (owner * 4 + zz * 2 + xh) * width
                at = pl.ds(pl.multiple_of(spot, width), width)
                gb[at, :TILE] = left.astype(BF16)
                gb[at, TILE:] = right.astype(BF16)

    def put(k, value, fresh=False):
        for part in range(TILE // PART):
            piece = value[part * PART : (part + 1) * PART, :]
            at = slice(k * PART, (k + 1) * PART)
            if fresh:
                corr[part, at, :] = piece
            else:
                corr[part, at, :] += piece

    flip = (iota((TILE, TILE), 0) + iota((TILE, TILE), 1) == TILE - 1).astype(BF16)
    turned = mm(f_ref[...], flip)
    t_ref[0] = jnp.zeros((TILE, TILE), BF16)

    def make_tile(k):
        before = turned[k - 1 : k] if k else jnp.zeros((1, TILE), F32)
        line = jnp.concatenate([before, turned[k : k + 1]], axis=1)
        spread = jnp.broadcast_to(line, (TILE, 2 * TILE))
        turn = pltpu.roll(spread, 1, 1, stride=1, stride_axis=0)
        t_ref[k + 1] = turn[:, :TILE].astype(BF16)

    full_x = jnp.concatenate([x_ref[s] for s in range(senders)], axis=1)
    for d in range(nb):
        make_tile(2 * d)
        make_tile(2 * d + 1)
        span = -(-(nb - d) * width // BLK) * BLK
        moved = gb[d * width : d * width + span, :]
        mid = t_ref[2 * d + 1]
        up = t_ref[2 * d + 2]
        down = t_ref[2 * d]
        tile = jnp.concatenate(
            [
                jnp.concatenate([mid, down], axis=1),
                jnp.concatenate([up, mid], axis=1),
            ],
            axis=0,
        )
        if d == 0:
            acc[...] = mm(moved, tile)
        else:
            acc[:span, :] += mm(moved, tile)
        prod = mm(full_x[:, :span], moved)
        put(2 * d, prod[:TILE, :TILE], fresh=d == 0)
        put(2 * d + 1, prod[:TILE, TILE:] + prod[TILE:, :TILE], fresh=True)
        put(2 * d + 2, prod[TILE:, TILE:], fresh=True)

    for s in range(senders):
        for k in range(8):
            a = (s * 4 + k // 2) * width
            lo = k % 2 * TILE
            o_ref[s, k * width : (k + 1) * width, :] = acc[
                a : a + width, lo : lo + TILE
            ].astype(BF16)

    lane = iota((PART, TILE), 1)
    turned = lane <= iota((PART, TILE), 0)
    spill = jnp.zeros((PART, TILE), F32)
    carry = jnp.zeros((1, TILE), F32)
    lines = []
    for k in range(2 * nb + 2):
        total = spill
        if k <= 2 * nb:
            low = corr[0, k * PART : (k + 1) * PART, :]
            spill = jnp.zeros((PART, TILE), F32)
            for part in range(1, TILE // PART):
                by = part * PART
                move = pltpu.roll(corr[part, k * PART : (k + 1) * PART, :], by, 1)
                low = low + jnp.where(lane >= by, move, 0.0)
                spill = spill + jnp.where(lane < by, move, 0.0)
            total = total + low
        move = pltpu.roll(total, 1, 1, stride=1, stride_axis=0)
        line = jnp.sum(jnp.where(turned, 0.0, move), axis=0, keepdims=True)
        if k >= 2:
            lines.append(line + carry)
        carry = jnp.sum(jnp.where(turned, move, 0.0), axis=0, keepdims=True)

    at = 8 * width
    for s in range(senders):
        full = jnp.concatenate(lines[s * TAIL : (s + 1) * TAIL], axis=0)
        first = full.astype(BF16)
        rest = full - first.astype(F32)
        second = rest.astype(BF16)
        third = (rest - second.astype(F32)).astype(BF16)
        o_ref[s, at : at + 2 * TAIL, :] = jnp.concatenate([first, second], axis=0)
        o_ref[s, at + 2 * TAIL :, :] = third


def convolve(spot, g, xt, taps):
    senders = g.shape[0] // 2
    width = g.shape[1]
    nb = 4 * senders
    top = nb * width
    return pl.pallas_call(
        conv_body,
        out_shape=jax.ShapeDtypeStruct((senders, 8 * width + 3 * TAIL, TILE), BF16),
        in_specs=[pl.BlockSpec(memory_space=pltpu.SMEM)]
        + [pl.BlockSpec(memory_space=pltpu.VMEM)] * 3,
        scratch_shapes=[
            pltpu.VMEM((top + BLK, BLK), BF16),
            pltpu.VMEM((top, BLK), F32),
            pltpu.VMEM((TILE // PART, (2 * nb + 1) * PART, TILE), F32),
            pltpu.VMEM((2 * nb + 1, TILE, TILE), BF16),
        ],
        name="convolve",
        compiler_params=params(),
        cost_estimate=cost(6 * 10**9, 4 * 10**6),
    )(spot, g, xt, taps)


def finish_body(m_ref, o_ref, f_ref):
    groups, rows, _ = m_ref.shape
    width = (rows - 3 * TAIL) // 8
    for k in range(8):
        at = slice(k * width, (k + 1) * width)
        for h in range(groups // 4):
            four = [m_ref[4 * h + i, at, :].astype(F32) for i in range(4)]
            flat = jnp.concatenate(four, axis=0)
            o_ref[k * TILE : (k + 1) * TILE, h * TILE : (h + 1) * TILE] = flat.T.astype(BF16)
    at = 8 * width
    for g in range(groups):
        both = m_ref[g, at : at + 2 * TAIL, :].astype(F32)
        total = both[:TAIL] + both[TAIL:] + m_ref[g, at + 2 * TAIL :, :].astype(F32)
        for j in range(TAIL):
            f_ref[g : g + 1, j * TILE : (j + 1) * TILE] = total[j : j + 1, :]


def finish(major):
    groups, rows, lanes = major.shape
    width = (rows - 3 * TAIL) // 8
    return pl.pallas_call(
        finish_body,
        out_shape=(
            jax.ShapeDtypeStruct((8 * lanes, groups * width), BF16),
            jax.ShapeDtypeStruct((groups, TAIL * lanes), F32),
        ),
        name="finish",
        compiler_params=params(),
        cost_estimate=cost(10**6, 4 * major.size),
    )(major)


def on_device(conv_input, grad_out, out_weight, filters):
    groups = filters.shape[0]
    width = conv_input.shape[1] // groups
    seq = ("y", "zlo")
    near = ("zlo", "zhi")
    x = lax.axis_index("x").astype(jnp.int32)
    core = lax.axis_index("core").astype(jnp.int32)
    zhi = lax.axis_index("zhi").astype(jnp.int32)
    half = grad_out.shape[0] // 2
    before = lax.ppermute(grad_out, "x", X_UP)
    after = lax.ppermute(grad_out, "x", X_DOWN)
    near_own = lax.ppermute(grad_out, near, Z_NEAR)
    other_weight = lax.ppermute(out_weight, "core", SWAP)
    far_a = lax.ppermute(before[:half], "x", X_UP)
    far_b = lax.ppermute(after[half:], "x", X_DOWN)
    turned = prep_input(conv_input, groups, width)
    turned = lax.all_to_all(turned, seq, 0, 0, tiled=True)
    near_before = lax.ppermute(near_own, "x", X_UP)
    near_after = lax.ppermute(near_own, "x", X_DOWN)
    near_far_a = lax.ppermute(far_a, near, Z_NEAR)
    near_far_b = lax.ppermute(far_b, near, Z_NEAR)
    taps = lax.dynamic_index_in_dim(filters, lax.axis_index(seq), 0, False)
    taps = taps.reshape(-1, TILE)
    spots = jnp.stack([x, core])
    shifts = [(0, 0), (3, 0), (1, 0), (2, 0), (2, half)]
    g = project(
        spots, out_weight, other_weight,
        [grad_out, before, after, far_a, far_b], shifts,
    )
    g = project(
        spots, out_weight, other_weight,
        [near_own, near_before, near_after, near_far_a, near_far_b], shifts, g,
    )
    g = g.reshape(2 * groups, width, -1)
    g = lax.all_to_all(g, ("core",) + seq, 0, 0, tiled=True)
    major = convolve(zhi.reshape(1), g, turned, taps)
    major = lax.all_to_all(major, seq, 0, 0, tiled=True)
    return finish(major)


def solution(mesh):
    fine = Mesh(
        mesh.devices.reshape(4, 2, 2, 4, 2),
        ("y", "zlo", "zhi", "x", "core"),
        axis_types=(jax.sharding.AxisType.Auto,) * 5,
    )
    seq = ("y", "zlo")
    chan = ("zhi", "x", "core")
    in_specs = (P(seq, chan), P(seq + chan, None), P(chan, None), P(chan, None))
    out_specs = (P(seq, chan), P(chan, seq))
    return jax.shard_map(
        on_device, mesh=fine, in_specs=in_specs, out_specs=out_specs, check_vma=False
    )
```

```python
import functools

import jax
import jax.numpy as jnp
from jax import lax
from jax.experimental import pallas as pl
from jax.experimental.pallas import tpu as pltpu
from jax.sharding import Mesh
from jax.sharding import PartitionSpec as P

F32 = jnp.float32
BF16 = jnp.bfloat16

TILE = 128
BLK = 256
PART = 16
TAIL = 8
STEP = 1024
EARLY = 56
VMEM_MIB = 24
X_UP = [(i, (i + 1) % 4) for i in range(4)]
X_DOWN = [(i, (i - 1) % 4) for i in range(4)]
Z_NEAR = [(i, 3 - i) for i in range(4)]
SWAP = [(0, 1), (1, 0)]


def mm(a, b, dims=(((1,), (0,)), ((), ()))):
    return lax.dot_general(a, b, dims, preferred_element_type=F32)


def iota(shape, axis):
    return lax.broadcasted_iota(jnp.int32, shape, axis)


def params():
    return pltpu.CompilerParams(vmem_limit_bytes=VMEM_MIB * 2**20)


def cost(flops, moved):
    return pl.CostEstimate(flops=flops, bytes_accessed=moved, transcendentals=0)


def prep_body(x_ref, o_ref, *, groups, width):
    blocks = x_ref.shape[0] // BLK
    chans = x_ref.shape[1]
    flip = (iota((BLK, BLK), 0) + iota((BLK, BLK), 1) == BLK - 1).astype(BF16)
    turned = [
        mm(flip, x_ref[a * BLK : (a + 1) * BLK, :]).astype(BF16) for a in range(blocks)
    ]
    row = iota((chans, TILE), 0)
    col = iota((chans, TILE), 1)
    for g in range(groups):
        total = jnp.zeros((BLK, TILE), F32)
        for a in range(blocks):
            pick = (row - g * width == col - a * width) & (col // width == a)
            total = total + mm(turned[a], pick.astype(BF16))
        o_ref[g] = total.astype(BF16)


def prep_input(x, groups, width):
    return pl.pallas_call(
        functools.partial(prep_body, groups=groups, width=width),
        out_shape=jax.ShapeDtypeStruct((groups, BLK, TILE), BF16),
        name="prep_input",
        compiler_params=params(),
        cost_estimate=cost(2 * 10**9, 4 * x.size),
    )(x)


def turn_taps(f_ref):
    flip = (iota((TILE, TILE), 0) + iota((TILE, TILE), 1) == TILE - 1).astype(BF16)
    return mm(f_ref[...], flip)


def toeplitz_tile(turned, k):
    before = turned[k - 1 : k] if k else jnp.zeros((1, TILE), F32)
    line = jnp.concatenate([before, turned[k : k + 1]], axis=1)
    spread = jnp.broadcast_to(line, (TILE, 2 * TILE))
    turn = pltpu.roll(spread, 1, 1, stride=1, stride_axis=0)
    return turn[:, :TILE].astype(BF16)


def ready_body(f_ref, x_ref, t_ref, y_ref):
    for s in range(x_ref.shape[0]):
        y_ref[:, s * TILE : (s + 1) * TILE] = x_ref[s]
    turned = turn_taps(f_ref)
    t_ref[0] = jnp.zeros((TILE, TILE), BF16)
    for k in range(t_ref.shape[0] - 1):
        t_ref[k + 1] = toeplitz_tile(turned, k)


def ready(taps, x):
    vmem = pl.BlockSpec(memory_space=pltpu.VMEM)
    return pl.pallas_call(
        ready_body,
        out_shape=(
            jax.ShapeDtypeStruct((EARLY, TILE, TILE), BF16),
            jax.ShapeDtypeStruct((BLK, x.shape[0] * TILE), BF16),
        ),
        in_specs=[vmem] * 2,
        out_specs=(vmem, vmem),
        name="ready",
        compiler_params=params(),
        cost_estimate=cost(2 * 10**9, 2 * EARLY * TILE * TILE),
    )(taps, x)


def multiply(s_ref, weights, blocks, shifts, o_ref, part, rows, acc, held, sem):
    x = s_ref[0]
    core = s_ref[1]
    chans, depth = weights[0].shape
    size = rows.shape[0] // 4
    for ref, (shift, at) in zip(blocks, shifts):
        spot = lax.rem(x + shift, 4) * size + at
        rows[pl.ds(pl.multiple_of(spot, 32), ref.shape[0]), :] = ref[...]
    dims = (((1,), (1,)), ((), ()))
    for k in range(depth // STEP):
        at = slice(k * STEP, (k + 1) * STEP)
        for half, ref in enumerate(weights):
            spot = slice(half * chans, (half + 1) * chans)
            value = mm(ref[:, at], rows[:, at], dims)
            if k:
                acc[spot, :] += value
            else:
                acc[spot, :] = value
    copies = []
    for half in range(2):
        held[half] = acc[half * chans : (half + 1) * chans, :].astype(BF16)
        to = core if half == 0 else 1 - core
        at = pl.ds(pl.multiple_of(to * chans, chans), chans)
        lanes = pl.ds(part * rows.shape[0], rows.shape[0])
        copies.append(
            pltpu.make_async_copy(held.at[half], o_ref.at[at, lanes], sem.at[half])
        )
        copies[-1].start()
    for copy in copies:
        copy.wait()


def first_body(s_ref, *refs, shifts):
    count = len(shifts)
    weights, blocks, later = refs[:2], refs[2 : 2 + count], refs[2 + count]
    o_ref, keep_ref, rows, acc, held, sem = refs[3 + count :]
    keep = pltpu.make_async_copy(later, keep_ref, sem.at[2])
    keep.start()
    multiply(s_ref, weights, blocks, shifts, o_ref, 0, rows, acc, held, sem)
    keep.wait()


def second_body(s_ref, *refs, shifts):
    count = len(shifts)
    weights, blocks = refs[:2], refs[2 : 2 + count]
    o_ref, rows, acc, held, sem = refs[3 + count :]
    multiply(s_ref, weights, blocks, shifts, o_ref, 1, rows, acc, held, sem)


def project(spots, own, other, blocks, shifts, later=None, g=None):
    chans, depth = own.shape
    rows = sum(b.shape[0] for b in blocks)
    whole = jax.ShapeDtypeStruct((2 * chans, 2 * rows), BF16)
    anywhere = pl.BlockSpec(memory_space=pl.ANY)
    vmem = pl.BlockSpec(memory_space=pltpu.VMEM)
    if g is None:
        body, extra, out = first_body, later, (whole, jax.ShapeDtypeStruct(later.shape, BF16))
        out_specs, aliases = (anywhere, vmem), {}
    else:
        body, extra, out = second_body, g, whole
        out_specs, aliases = anywhere, {3 + len(blocks): 0}
    return pl.pallas_call(
        functools.partial(body, shifts=shifts),
        out_shape=out,
        in_specs=[pl.BlockSpec(memory_space=pltpu.SMEM)]
        + [vmem] * (2 + len(blocks))
        + [anywhere],
        out_specs=out_specs,
        input_output_aliases=aliases,
        scratch_shapes=[
            pltpu.VMEM((rows, depth), BF16),
            pltpu.VMEM((2 * chans, rows), F32),
            pltpu.VMEM((2, chans, rows), BF16),
            pltpu.SemaphoreType.DMA((3,)),
        ],
        name="project",
        compiler_params=params(),
        cost_estimate=cost(4 * chans * rows * depth, 2 * depth * (2 * chans + rows)),
    )(spots, own, other, *blocks, extra)


def conv_body(s_ref, g_ref, x_ref, t_ref, f_ref, o_ref, gb, acc, corr, late):
    zhi = s_ref[2]
    width = g_ref.shape[1]
    senders = g_ref.shape[0] // 2
    nb = 4 * senders
    top = nb * width
    lane = iota((width, TILE), 1)
    gb[top:, :] = jnp.zeros((gb.shape[0] - top, BLK), BF16)
    for half in range(2):
        for s in range(senders):
            owner = s ^ half
            zz = 1 - zhi if half else zhi
            for xh in range(2):
                lo = (half * 2 + xh) * TILE
                a = g_ref[s, :, lo : lo + TILE].astype(F32)
                b = g_ref[senders + s, :, lo : lo + TILE].astype(F32)
                left = jnp.where(lane < 64, a, pltpu.roll(b, 64, 1))
                right = jnp.where(lane < 64, pltpu.roll(a, 64, 1), b)
                spot = (owner * 4 + zz * 2 + xh) * width
                at = pl.ds(pl.multiple_of(spot, width), width)
                gb[at, :TILE] = left.astype(BF16)
                gb[at, TILE:] = right.astype(BF16)

    def put(k, value, fresh=False):
        for part in range(TILE // PART):
            piece = value[part * PART : (part + 1) * PART, :]
            at = slice(k * PART, (k + 1) * PART)
            if fresh:
                corr[part, at, :] = piece
            else:
                corr[part, at, :] += piece

    turned = turn_taps(f_ref)

    def tile_at(index):
        return t_ref[index] if index < EARLY else late[index - EARLY]

    for d in range(nb):
        for k in (2 * d, 2 * d + 1):
            if k + 1 >= EARLY:
                late[k + 1 - EARLY] = toeplitz_tile(turned, k)
        span = -(-(nb - d) * width // BLK) * BLK
        moved = gb[d * width : d * width + span, :]
        mid = tile_at(2 * d + 1)
        up = tile_at(2 * d + 2)
        down = tile_at(2 * d)
        tile = jnp.concatenate(
            [
                jnp.concatenate([mid, down], axis=1),
                jnp.concatenate([up, mid], axis=1),
            ],
            axis=0,
        )
        if d == 0:
            acc[...] = mm(moved, tile)
        else:
            acc[:span, :] += mm(moved, tile)
        prod = mm(x_ref[:, :span], moved)
        put(2 * d, prod[:TILE, :TILE], fresh=d == 0)
        put(2 * d + 1, prod[:TILE, TILE:] + prod[TILE:, :TILE], fresh=True)
        put(2 * d + 2, prod[TILE:, TILE:], fresh=True)

    for s in range(senders):
        for k in range(8):
            a = (s * 4 + k // 2) * width
            lo = k % 2 * TILE
            o_ref[s, k * width : (k + 1) * width, :] = acc[
                a : a + width, lo : lo + TILE
            ].astype(BF16)

    lane = iota((PART, TILE), 1)
    turned = lane <= iota((PART, TILE), 0)
    spill = jnp.zeros((PART, TILE), F32)
    carry = jnp.zeros((1, TILE), F32)
    lines = []
    for k in range(2 * nb + 2):
        total = spill
        if k <= 2 * nb:
            low = corr[0, k * PART : (k + 1) * PART, :]
            spill = jnp.zeros((PART, TILE), F32)
            for part in range(1, TILE // PART):
                by = part * PART
                move = pltpu.roll(corr[part, k * PART : (k + 1) * PART, :], by, 1)
                low = low + jnp.where(lane >= by, move, 0.0)
                spill = spill + jnp.where(lane < by, move, 0.0)
            total = total + low
        move = pltpu.roll(total, 1, 1, stride=1, stride_axis=0)
        line = jnp.sum(jnp.where(turned, 0.0, move), axis=0, keepdims=True)
        if k >= 2:
            lines.append(line + carry)
        carry = jnp.sum(jnp.where(turned, move, 0.0), axis=0, keepdims=True)

    at = 8 * width
    for s in range(senders):
        full = jnp.concatenate(lines[s * TAIL : (s + 1) * TAIL], axis=0)
        first = full.astype(BF16)
        rest = full - first.astype(F32)
        second = rest.astype(BF16)
        third = (rest - second.astype(F32)).astype(BF16)
        o_ref[s, at : at + 2 * TAIL, :] = jnp.concatenate([first, second], axis=0)
        o_ref[s, at + 2 * TAIL :, :] = third


def convolve(spot, g, xt, tiles, taps):
    senders = g.shape[0] // 2
    width = g.shape[1]
    nb = 4 * senders
    top = nb * width
    return pl.pallas_call(
        conv_body,
        out_shape=jax.ShapeDtypeStruct((senders, 8 * width + 3 * TAIL, TILE), BF16),
        in_specs=[pl.BlockSpec(memory_space=pltpu.SMEM)]
        + [pl.BlockSpec(memory_space=pltpu.VMEM)] * 4,
        scratch_shapes=[
            pltpu.VMEM((top + BLK, BLK), BF16),
            pltpu.VMEM((top, BLK), F32),
            pltpu.VMEM((TILE // PART, (2 * nb + 1) * PART, TILE), F32),
            pltpu.VMEM((2 * nb + 1 - EARLY, TILE, TILE), BF16),
        ],
        name="convolve",
        compiler_params=params(),
        cost_estimate=cost(6 * 10**9, 4 * 10**6),
    )(spot, g, xt, tiles, taps)


def finish_body(m_ref, o_ref, f_ref):
    groups, rows, _ = m_ref.shape
    width = (rows - 3 * TAIL) // 8
    for k in range(8):
        at = slice(k * width, (k + 1) * width)
        for h in range(groups // 4):
            four = [m_ref[4 * h + i, at, :].astype(F32) for i in range(4)]
            flat = jnp.concatenate(four, axis=0)
            o_ref[k * TILE : (k + 1) * TILE, h * TILE : (h + 1) * TILE] = flat.T.astype(BF16)
    at = 8 * width
    for g in range(groups):
        both = m_ref[g, at : at + 2 * TAIL, :].astype(F32)
        total = both[:TAIL] + both[TAIL:] + m_ref[g, at + 2 * TAIL :, :].astype(F32)
        for j in range(TAIL):
            f_ref[g : g + 1, j * TILE : (j + 1) * TILE] = total[j : j + 1, :]


def finish(major):
    groups, rows, lanes = major.shape
    width = (rows - 3 * TAIL) // 8
    return pl.pallas_call(
        finish_body,
        out_shape=(
            jax.ShapeDtypeStruct((8 * lanes, groups * width), BF16),
            jax.ShapeDtypeStruct((groups, TAIL * lanes), F32),
        ),
        name="finish",
        compiler_params=params(),
        cost_estimate=cost(10**6, 4 * major.size),
    )(major)


def on_device(conv_input, grad_out, out_weight, filters):
    groups = filters.shape[0]
    width = conv_input.shape[1] // groups
    seq = ("y", "zlo")
    near = ("zlo", "zhi")
    x = lax.axis_index("x").astype(jnp.int32)
    core = lax.axis_index("core").astype(jnp.int32)
    zhi = lax.axis_index("zhi").astype(jnp.int32)
    half = grad_out.shape[0] // 2
    spots = jnp.stack([x, core, zhi])
    spots, grad_out = lax.optimization_barrier((spots, grad_out))
    before = lax.ppermute(grad_out, "x", X_UP)
    after = lax.ppermute(grad_out, "x", X_DOWN)
    near_own = lax.ppermute(grad_out, near, Z_NEAR)
    other_weight = lax.ppermute(out_weight, "core", SWAP)
    far_a = lax.ppermute(before[:half], "x", X_UP)
    far_b = lax.ppermute(after[half:], "x", X_DOWN)
    turned = prep_input(conv_input, groups, width)
    turned = lax.all_to_all(turned, seq, 0, 0, tiled=True)
    near_before = lax.ppermute(near_own, "x", X_UP)
    near_after = lax.ppermute(near_own, "x", X_DOWN)
    near_far_a = lax.ppermute(far_a, near, Z_NEAR)
    near_far_b = lax.ppermute(far_b, near, Z_NEAR)
    taps = lax.dynamic_index_in_dim(filters, lax.axis_index(seq), 0, False)
    taps = taps.reshape(-1, TILE)
    tiles, xt = ready(taps, turned)
    shifts = [(0, 0), (3, 0), (1, 0), (2, 0), (2, half)]
    g, near_own = project(
        spots, out_weight, other_weight,
        [grad_out, before, after, far_a, far_b], shifts, later=near_own,
    )
    g = project(
        spots, out_weight, other_weight,
        [near_own, near_before, near_after, near_far_a, near_far_b], shifts, g=g,
    )
    g = g.reshape(2 * groups, width, -1)
    g = lax.all_to_all(g, ("core",) + seq, 0, 0, tiled=True)
    major = convolve(spots, g, xt, tiles, taps)
    major = lax.all_to_all(major, seq, 0, 0, tiled=True)
    return finish(major)


def solution(mesh):
    fine = Mesh(
        mesh.devices.reshape(4, 2, 2, 4, 2),
        ("y", "zlo", "zhi", "x", "core"),
        axis_types=(jax.sharding.AxisType.Auto,) * 5,
    )
    seq = ("y", "zlo")
    chan = ("zhi", "x", "core")
    in_specs = (P(seq, chan), P(seq + chan, None), P(chan, None), P(chan, None))
    out_specs = (P(seq, chan), P(chan, seq))
    return jax.shard_map(
        on_device, mesh=fine, in_specs=in_specs, out_specs=out_specs, check_vma=False
    )
```

```python
import functools

import jax
import jax.numpy as jnp
from jax import lax
from jax.experimental import pallas as pl
from jax.experimental.pallas import tpu as pltpu
from jax.sharding import Mesh
from jax.sharding import PartitionSpec as P

F32 = jnp.float32
BF16 = jnp.bfloat16

TILE = 128
BLK = 256
PART = 16
TAIL = 8
STEP = 1024
EARLY = 56
BATCH = 2
VMEM_MIB = 24
X_UP = [(i, (i + 1) % 4) for i in range(4)]
X_DOWN = [(i, (i - 1) % 4) for i in range(4)]
Z_NEAR = [(i, 3 - i) for i in range(4)]
SWAP = [(0, 1), (1, 0)]


def mm(a, b, dims=(((1,), (0,)), ((), ()))):
    return lax.dot_general(a, b, dims, preferred_element_type=F32)


def iota(shape, axis):
    return lax.broadcasted_iota(jnp.int32, shape, axis)


def params():
    return pltpu.CompilerParams(vmem_limit_bytes=VMEM_MIB * 2**20)


def cost(flops, moved):
    return pl.CostEstimate(flops=flops, bytes_accessed=moved, transcendentals=0)


def prep_body(x_ref, o_ref, *, groups, width):
    blocks = x_ref.shape[0] // BLK
    chans = x_ref.shape[1]
    flip = (iota((BLK, BLK), 0) + iota((BLK, BLK), 1) == BLK - 1).astype(BF16)
    turned = [
        mm(flip, x_ref[a * BLK : (a + 1) * BLK, :]).astype(BF16) for a in range(blocks)
    ]
    row = iota((chans, TILE), 0)
    col = iota((chans, TILE), 1)
    for g in range(groups):
        total = jnp.zeros((BLK, TILE), F32)
        for a in range(blocks):
            pick = (row - g * width == col - a * width) & (col // width == a)
            total = total + mm(turned[a], pick.astype(BF16))
        o_ref[g] = total.astype(BF16)


def prep_input(x, groups, width):
    return pl.pallas_call(
        functools.partial(prep_body, groups=groups, width=width),
        out_shape=jax.ShapeDtypeStruct((groups, BLK, TILE), BF16),
        name="prep_input",
        compiler_params=params(),
        cost_estimate=cost(2 * 10**9, 4 * x.size),
    )(x)


def turn_taps(f_ref):
    flip = (iota((TILE, TILE), 0) + iota((TILE, TILE), 1) == TILE - 1).astype(BF16)
    return mm(f_ref[...], flip)


def toeplitz_tile(turned, k):
    before = turned[k - 1 : k] if k else jnp.zeros((1, TILE), F32)
    line = jnp.concatenate([before, turned[k : k + 1]], axis=1)
    spread = jnp.broadcast_to(line, (TILE, 2 * TILE))
    turn = pltpu.roll(spread, 1, 1, stride=1, stride_axis=0)
    return turn[:, :TILE].astype(BF16)


def ready_body(f_ref, x_ref, t_ref, y_ref):
    for s in range(x_ref.shape[0]):
        y_ref[:, s * TILE : (s + 1) * TILE] = x_ref[s]
    turned = turn_taps(f_ref)
    t_ref[0] = jnp.zeros((TILE, TILE), BF16)
    for k in range(t_ref.shape[0] - 1):
        t_ref[k + 1] = toeplitz_tile(turned, k)


def ready(taps, x):
    vmem = pl.BlockSpec(memory_space=pltpu.VMEM)
    return pl.pallas_call(
        ready_body,
        out_shape=(
            jax.ShapeDtypeStruct((EARLY, TILE, TILE), BF16),
            jax.ShapeDtypeStruct((BLK, x.shape[0] * TILE), BF16),
        ),
        in_specs=[vmem] * 2,
        out_specs=(vmem, vmem),
        name="ready",
        compiler_params=params(),
        cost_estimate=cost(2 * 10**9, 2 * EARLY * TILE * TILE),
    )(taps, x)


def multiply(s_ref, weights, blocks, shifts, o_ref, part, rows, acc, held, sem):
    x = s_ref[0]
    core = s_ref[1]
    chans, depth = weights[0].shape
    size = rows.shape[0] // 4
    for ref, (shift, at) in zip(blocks, shifts):
        spot = lax.rem(x + shift, 4) * size + at
        rows[pl.ds(pl.multiple_of(spot, 32), ref.shape[0]), :] = ref[...]
    dims = (((1,), (1,)), ((), ()))
    for k in range(depth // STEP):
        at = slice(k * STEP, (k + 1) * STEP)
        for half, ref in enumerate(weights):
            spot = slice(half * chans, (half + 1) * chans)
            value = mm(ref[:, at], rows[:, at], dims)
            if k:
                acc[spot, :] += value
            else:
                acc[spot, :] = value
    copies = []
    for half in range(2):
        held[half] = acc[half * chans : (half + 1) * chans, :].astype(BF16)
        to = core if half == 0 else 1 - core
        at = pl.ds(pl.multiple_of(to * chans, chans), chans)
        lanes = pl.ds(part * rows.shape[0], rows.shape[0])
        copies.append(
            pltpu.make_async_copy(held.at[half], o_ref.at[at, lanes], sem.at[half])
        )
        copies[-1].start()
    for copy in copies:
        copy.wait()


def first_body(s_ref, *refs, shifts):
    count = len(shifts)
    weights, blocks, later = refs[:2], refs[2 : 2 + count], refs[2 + count]
    o_ref, keep_ref, rows, acc, held, sem = refs[3 + count :]
    keep = pltpu.make_async_copy(later, keep_ref, sem.at[2])
    keep.start()
    multiply(s_ref, weights, blocks, shifts, o_ref, 0, rows, acc, held, sem)
    keep.wait()


def second_body(s_ref, *refs, shifts):
    count = len(shifts)
    weights, blocks = refs[:2], refs[2 : 2 + count]
    o_ref, rows, acc, held, sem = refs[3 + count :]
    multiply(s_ref, weights, blocks, shifts, o_ref, 1, rows, acc, held, sem)


def project(spots, own, other, blocks, shifts, later=None, g=None):
    chans, depth = own.shape
    rows = sum(b.shape[0] for b in blocks)
    whole = jax.ShapeDtypeStruct((2 * chans, 2 * rows), BF16)
    anywhere = pl.BlockSpec(memory_space=pl.ANY)
    vmem = pl.BlockSpec(memory_space=pltpu.VMEM)
    if g is None:
        body, extra, out = first_body, later, (whole, jax.ShapeDtypeStruct(later.shape, BF16))
        out_specs, aliases = (anywhere, vmem), {}
    else:
        body, extra, out = second_body, g, whole
        out_specs, aliases = anywhere, {3 + len(blocks): 0}
    return pl.pallas_call(
        functools.partial(body, shifts=shifts),
        out_shape=out,
        in_specs=[pl.BlockSpec(memory_space=pltpu.SMEM)]
        + [vmem] * (2 + len(blocks))
        + [anywhere],
        out_specs=out_specs,
        input_output_aliases=aliases,
        scratch_shapes=[
            pltpu.VMEM((rows, depth), BF16),
            pltpu.VMEM((2 * chans, rows), F32),
            pltpu.VMEM((2, chans, rows), BF16),
            pltpu.SemaphoreType.DMA((3,)),
        ],
        name="project",
        compiler_params=params(),
        cost_estimate=cost(4 * chans * rows * depth, 2 * depth * (2 * chans + rows)),
    )(spots, own, other, *blocks, extra)


def conv_body(s_ref, g_ref, x_ref, t_ref, f_ref, o_ref, gb, acc, corr, late):
    zhi = s_ref[2]
    width = g_ref.shape[1]
    senders = g_ref.shape[0] // 2
    nb = 4 * senders
    top = nb * width
    lane = iota((width, TILE), 1)
    gb[top:, :] = jnp.zeros((gb.shape[0] - top, BLK), BF16)
    for half in range(2):
        for s in range(senders):
            owner = s ^ half
            zz = 1 - zhi if half else zhi
            for xh in range(2):
                lo = (half * 2 + xh) * TILE
                a = g_ref[s, :, lo : lo + TILE].astype(F32)
                b = g_ref[senders + s, :, lo : lo + TILE].astype(F32)
                left = jnp.where(lane < 64, a, pltpu.roll(b, 64, 1))
                right = jnp.where(lane < 64, pltpu.roll(a, 64, 1), b)
                spot = (owner * 4 + zz * 2 + xh) * width
                at = pl.ds(pl.multiple_of(spot, width), width)
                gb[at, :TILE] = left.astype(BF16)
                gb[at, TILE:] = right.astype(BF16)

    def put(k, value, fresh=False):
        for part in range(TILE // PART):
            piece = value[part * PART : (part + 1) * PART, :]
            at = slice(k * PART, (k + 1) * PART)
            if fresh:
                corr[part, at, :] = piece
            else:
                corr[part, at, :] += piece

    turned = turn_taps(f_ref)

    def tile_at(index):
        return t_ref[index] if index < EARLY else late[index - EARLY]

    def block_tile(d):
        for k in (2 * d, 2 * d + 1):
            if k + 1 >= EARLY:
                late[k + 1 - EARLY] = toeplitz_tile(turned, k)
        mid = tile_at(2 * d + 1)
        up = tile_at(2 * d + 2)
        down = tile_at(2 * d)
        return jnp.concatenate(
            [
                jnp.concatenate([mid, down], axis=1),
                jnp.concatenate([up, mid], axis=1),
            ],
            axis=0,
        )

    for d in range(nb):
        span = -(-(nb - d) * width // BLK) * BLK
        if d % BATCH == 0:
            many = range(d, d + BATCH)
            moved = [gb[e * width : e * width + span, :] for e in many]
            value = mm(
                jnp.concatenate(moved, axis=1),
                jnp.concatenate([block_tile(e) for e in many], axis=0),
            )
            if d == 0:
                acc[...] = value
            else:
                acc[:span, :] += value
        prod = mm(x_ref[:, :span], gb[d * width : d * width + span, :])
        put(2 * d, prod[:TILE, :TILE], fresh=d == 0)
        put(2 * d + 1, prod[:TILE, TILE:] + prod[TILE:, :TILE], fresh=True)
        put(2 * d + 2, prod[TILE:, TILE:], fresh=True)

    for s in range(senders):
        for k in range(8):
            a = (s * 4 + k // 2) * width
            lo = k % 2 * TILE
            o_ref[s, k * width : (k + 1) * width, :] = acc[
                a : a + width, lo : lo + TILE
            ].astype(BF16)

    lane = iota((PART, TILE), 1)
    turned = lane <= iota((PART, TILE), 0)
    spill = jnp.zeros((PART, TILE), F32)
    carry = jnp.zeros((1, TILE), F32)
    lines = []
    for k in range(2 * nb + 2):
        total = spill
        if k <= 2 * nb:
            low = corr[0, k * PART : (k + 1) * PART, :]
            spill = jnp.zeros((PART, TILE), F32)
            for part in range(1, TILE // PART):
                by = part * PART
                move = pltpu.roll(corr[part, k * PART : (k + 1) * PART, :], by, 1)
                low = low + jnp.where(lane >= by, move, 0.0)
                spill = spill + jnp.where(lane < by, move, 0.0)
            total = total + low
        move = pltpu.roll(total, 1, 1, stride=1, stride_axis=0)
        line = jnp.sum(jnp.where(turned, 0.0, move), axis=0, keepdims=True)
        if k >= 2:
            lines.append(line + carry)
        carry = jnp.sum(jnp.where(turned, move, 0.0), axis=0, keepdims=True)

    at = 8 * width
    for s in range(senders):
        full = jnp.concatenate(lines[s * TAIL : (s + 1) * TAIL], axis=0)
        first = full.astype(BF16)
        rest = full - first.astype(F32)
        second = rest.astype(BF16)
        third = (rest - second.astype(F32)).astype(BF16)
        o_ref[s, at : at + 2 * TAIL, :] = jnp.concatenate([first, second], axis=0)
        o_ref[s, at + 2 * TAIL :, :] = third


def convolve(spot, g, xt, tiles, taps):
    senders = g.shape[0] // 2
    width = g.shape[1]
    nb = 4 * senders
    top = nb * width
    return pl.pallas_call(
        conv_body,
        out_shape=jax.ShapeDtypeStruct((senders, 8 * width + 3 * TAIL, TILE), BF16),
        in_specs=[pl.BlockSpec(memory_space=pltpu.SMEM)]
        + [pl.BlockSpec(memory_space=pltpu.VMEM)] * 4,
        scratch_shapes=[
            pltpu.VMEM((top + 2 * BLK, BLK), BF16),
            pltpu.VMEM((top, BLK), F32),
            pltpu.VMEM((TILE // PART, (2 * nb + 1) * PART, TILE), F32),
            pltpu.VMEM((2 * nb + 1 - EARLY, TILE, TILE), BF16),
        ],
        name="convolve",
        compiler_params=params(),
        cost_estimate=cost(6 * 10**9, 4 * 10**6),
    )(spot, g, xt, tiles, taps)


def finish_body(m_ref, o_ref, f_ref):
    groups, rows, _ = m_ref.shape
    width = (rows - 3 * TAIL) // 8
    for k in range(8):
        at = slice(k * width, (k + 1) * width)
        for h in range(groups // 4):
            four = [m_ref[4 * h + i, at, :].astype(F32) for i in range(4)]
            flat = jnp.concatenate(four, axis=0)
            o_ref[k * TILE : (k + 1) * TILE, h * TILE : (h + 1) * TILE] = flat.T.astype(BF16)
    at = 8 * width
    for g in range(groups):
        both = m_ref[g, at : at + 2 * TAIL, :].astype(F32)
        total = both[:TAIL] + both[TAIL:] + m_ref[g, at + 2 * TAIL :, :].astype(F32)
        for j in range(TAIL):
            f_ref[g : g + 1, j * TILE : (j + 1) * TILE] = total[j : j + 1, :]


def finish(major):
    groups, rows, lanes = major.shape
    width = (rows - 3 * TAIL) // 8
    return pl.pallas_call(
        finish_body,
        out_shape=(
            jax.ShapeDtypeStruct((8 * lanes, groups * width), BF16),
            jax.ShapeDtypeStruct((groups, TAIL * lanes), F32),
        ),
        name="finish",
        compiler_params=params(),
        cost_estimate=cost(10**6, 4 * major.size),
    )(major)


def on_device(conv_input, grad_out, out_weight, filters):
    groups = filters.shape[0]
    width = conv_input.shape[1] // groups
    seq = ("y", "zlo")
    near = ("zlo", "zhi")
    x = lax.axis_index("x").astype(jnp.int32)
    core = lax.axis_index("core").astype(jnp.int32)
    zhi = lax.axis_index("zhi").astype(jnp.int32)
    half = grad_out.shape[0] // 2
    spots = jnp.stack([x, core, zhi])
    spots, grad_out = lax.optimization_barrier((spots, grad_out))
    before = lax.ppermute(grad_out, "x", X_UP)
    after = lax.ppermute(grad_out, "x", X_DOWN)
    near_own = lax.ppermute(grad_out, near, Z_NEAR)
    other_weight = lax.ppermute(out_weight, "core", SWAP)
    far_a = lax.ppermute(before[:half], "x", X_UP)
    far_b = lax.ppermute(after[half:], "x", X_DOWN)
    turned = prep_input(conv_input, groups, width)
    turned = lax.all_to_all(turned, seq, 0, 0, tiled=True)
    near_before = lax.ppermute(near_own, "x", X_UP)
    near_after = lax.ppermute(near_own, "x", X_DOWN)
    near_far_a = lax.ppermute(far_a, near, Z_NEAR)
    near_far_b = lax.ppermute(far_b, near, Z_NEAR)
    taps = lax.dynamic_index_in_dim(filters, lax.axis_index(seq), 0, False)
    taps = taps.reshape(-1, TILE)
    tiles, xt = ready(taps, turned)
    shifts = [(0, 0), (3, 0), (1, 0), (2, 0), (2, half)]
    g, near_own = project(
        spots, out_weight, other_weight,
        [grad_out, before, after, far_a, far_b], shifts, later=near_own,
    )
    g = project(
        spots, out_weight, other_weight,
        [near_own, near_before, near_after, near_far_a, near_far_b], shifts, g=g,
    )
    g = g.reshape(2 * groups, width, -1)
    g = lax.all_to_all(g, ("core",) + seq, 0, 0, tiled=True)
    major = convolve(spots, g, xt, tiles, taps)
    major = lax.all_to_all(major, seq, 0, 0, tiled=True)
    return finish(major)


def solution(mesh):
    fine = Mesh(
        mesh.devices.reshape(4, 2, 2, 4, 2),
        ("y", "zlo", "zhi", "x", "core"),
        axis_types=(jax.sharding.AxisType.Auto,) * 5,
    )
    seq = ("y", "zlo")
    chan = ("zhi", "x", "core")
    in_specs = (P(seq, chan), P(seq + chan, None), P(chan, None), P(chan, None))
    out_specs = (P(seq, chan), P(chan, seq))
    return jax.shard_map(
        on_device, mesh=fine, in_specs=in_specs, out_specs=out_specs, check_vma=False
    )
```

```python
import functools

import jax
import jax.numpy as jnp
from jax import lax
from jax.experimental import pallas as pl
from jax.experimental.pallas import tpu as pltpu
from jax.sharding import Mesh
from jax.sharding import PartitionSpec as P

F32 = jnp.float32
BF16 = jnp.bfloat16

TILE = 128
BLK = 256
PART = 16
TAIL = 8
STEP = 1024
EARLY = 56
VMEM_MIB = 24
X_UP = [(i, (i + 1) % 4) for i in range(4)]
X_DOWN = [(i, (i - 1) % 4) for i in range(4)]
Z_NEAR = [(i, 3 - i) for i in range(4)]
SWAP = [(0, 1), (1, 0)]


def mm(a, b, dims=(((1,), (0,)), ((), ()))):
    return lax.dot_general(a, b, dims, preferred_element_type=F32)


def iota(shape, axis):
    return lax.broadcasted_iota(jnp.int32, shape, axis)


def params():
    return pltpu.CompilerParams(vmem_limit_bytes=VMEM_MIB * 2**20)


def cost(flops, moved):
    return pl.CostEstimate(flops=flops, bytes_accessed=moved, transcendentals=0)


def prep_body(x_ref, o_ref, *, groups, width):
    blocks = x_ref.shape[0] // BLK
    chans = x_ref.shape[1]
    flip = (iota((BLK, BLK), 0) + iota((BLK, BLK), 1) == BLK - 1).astype(BF16)
    turned = [
        mm(flip, x_ref[a * BLK : (a + 1) * BLK, :]).astype(BF16) for a in range(blocks)
    ]
    row = iota((chans, TILE), 0)
    col = iota((chans, TILE), 1)
    for g in range(groups):
        total = jnp.zeros((BLK, TILE), F32)
        for a in range(blocks):
            pick = (row - g * width == col - a * width) & (col // width == a)
            total = total + mm(turned[a], pick.astype(BF16))
        o_ref[g] = total.astype(BF16)


def prep_input(x, groups, width):
    return pl.pallas_call(
        functools.partial(prep_body, groups=groups, width=width),
        out_shape=jax.ShapeDtypeStruct((groups, BLK, TILE), BF16),
        name="prep_input",
        compiler_params=params(),
        cost_estimate=cost(2 * 10**9, 4 * x.size),
    )(x)


def turn_taps(f_ref):
    flip = (iota((TILE, TILE), 0) + iota((TILE, TILE), 1) == TILE - 1).astype(BF16)
    return mm(f_ref[...], flip)


def toeplitz_tile(turned, k):
    before = turned[k - 1 : k] if k else jnp.zeros((1, TILE), F32)
    line = jnp.concatenate([before, turned[k : k + 1]], axis=1)
    spread = jnp.broadcast_to(line, (TILE, 2 * TILE))
    turn = pltpu.roll(spread, 1, 1, stride=1, stride_axis=0)
    return turn[:, :TILE].astype(BF16)


def ready_body(f_ref, x_ref, t_ref, y_ref):
    for s in range(x_ref.shape[0]):
        y_ref[:, s * TILE : (s + 1) * TILE] = x_ref[s]
    turned = turn_taps(f_ref)
    t_ref[0] = jnp.zeros((TILE, TILE), BF16)
    for k in range(t_ref.shape[0] - 1):
        t_ref[k + 1] = toeplitz_tile(turned, k)


def ready(taps, x):
    vmem = pl.BlockSpec(memory_space=pltpu.VMEM)
    return pl.pallas_call(
        ready_body,
        out_shape=(
            jax.ShapeDtypeStruct((EARLY, TILE, TILE), BF16),
            jax.ShapeDtypeStruct((BLK, x.shape[0] * TILE), BF16),
        ),
        in_specs=[vmem] * 2,
        out_specs=(vmem, vmem),
        name="ready",
        compiler_params=params(),
        cost_estimate=cost(2 * 10**9, 2 * EARLY * TILE * TILE),
    )(taps, x)


def multiply(s_ref, weights, blocks, shifts, o_ref, part, rows, held, sem):
    x = s_ref[0]
    core = s_ref[1]
    chans, depth = weights[0].shape
    size = rows.shape[0] // 4
    for ref, (shift, at) in zip(blocks, shifts):
        spot = lax.rem(x + shift, 4) * size + at
        rows[pl.ds(pl.multiple_of(spot, 32), ref.shape[0]), :] = ref[...]
    dims = (((1,), (1,)), ((), ()))
    lanes = pl.ds(part * rows.shape[0], rows.shape[0])
    copies = []
    for half, ref in enumerate(weights):
        total = mm(ref[:, :STEP], rows[:, :STEP], dims)
        for k in range(1, depth // STEP):
            at = slice(k * STEP, (k + 1) * STEP)
            total = total + mm(ref[:, at], rows[:, at], dims)
        held[half] = total.astype(BF16)
        to = core if half == 0 else 1 - core
        at = pl.ds(pl.multiple_of(to * chans, chans), chans)
        copies.append(
            pltpu.make_async_copy(held.at[half], o_ref.at[at, lanes], sem.at[half])
        )
        copies[-1].start()
    for copy in copies:
        copy.wait()


def first_body(s_ref, *refs, shifts):
    count = len(shifts)
    weights, blocks, later = refs[:2], refs[2 : 2 + count], refs[2 + count]
    o_ref, keep_ref, rows, held, sem = refs[3 + count :]
    keep = pltpu.make_async_copy(later, keep_ref, sem.at[2])
    keep.start()
    multiply(s_ref, weights, blocks, shifts, o_ref, 0, rows, held, sem)
    keep.wait()


def second_body(s_ref, *refs, shifts):
    count = len(shifts)
    weights, blocks = refs[:2], refs[2 : 2 + count]
    o_ref, rows, held, sem = refs[3 + count :]
    multiply(s_ref, weights, blocks, shifts, o_ref, 1, rows, held, sem)


def project(spots, own, other, blocks, shifts, later=None, g=None):
    chans, depth = own.shape
    rows = sum(b.shape[0] for b in blocks)
    whole = jax.ShapeDtypeStruct((2 * chans, 2 * rows), BF16)
    anywhere = pl.BlockSpec(memory_space=pl.ANY)
    vmem = pl.BlockSpec(memory_space=pltpu.VMEM)
    if g is None:
        body, extra, out = first_body, later, (whole, jax.ShapeDtypeStruct(later.shape, BF16))
        out_specs, aliases = (anywhere, vmem), {}
    else:
        body, extra, out = second_body, g, whole
        out_specs, aliases = anywhere, {3 + len(blocks): 0}
    return pl.pallas_call(
        functools.partial(body, shifts=shifts),
        out_shape=out,
        in_specs=[pl.BlockSpec(memory_space=pltpu.SMEM)]
        + [vmem] * (2 + len(blocks))
        + [anywhere],
        out_specs=out_specs,
        input_output_aliases=aliases,
        scratch_shapes=[
            pltpu.VMEM((rows, depth), BF16),
            pltpu.VMEM((2, chans, rows), BF16),
            pltpu.SemaphoreType.DMA((3,)),
        ],
        name="project",
        compiler_params=params(),
        cost_estimate=cost(4 * chans * rows * depth, 2 * depth * (2 * chans + rows)),
    )(spots, own, other, *blocks, extra)


def conv_body(s_ref, g_ref, x_ref, t_ref, f_ref, o_ref, gb, acc, corr, late):
    zhi = s_ref[2]
    width = g_ref.shape[1]
    senders = g_ref.shape[0] // 2
    nb = 4 * senders
    top = nb * width
    lane = iota((width, TILE), 1)
    gb[top:, :] = jnp.zeros((gb.shape[0] - top, BLK), BF16)
    for half in range(2):
        for s in range(senders):
            owner = s ^ half
            zz = 1 - zhi if half else zhi
            for xh in range(2):
                lo = (half * 2 + xh) * TILE
                a = g_ref[s, :, lo : lo + TILE].astype(F32)
                b = g_ref[senders + s, :, lo : lo + TILE].astype(F32)
                left = jnp.where(lane < 64, a, pltpu.roll(b, 64, 1))
                right = jnp.where(lane < 64, pltpu.roll(a, 64, 1), b)
                spot = (owner * 4 + zz * 2 + xh) * width
                at = pl.ds(pl.multiple_of(spot, width), width)
                gb[at, :TILE] = left.astype(BF16)
                gb[at, TILE:] = right.astype(BF16)

    def put(k, value, fresh=False):
        for part in range(TILE // PART):
            piece = value[part * PART : (part + 1) * PART, :]
            at = slice(k * PART, (k + 1) * PART)
            if fresh:
                corr[part, at, :] = piece
            else:
                corr[part, at, :] += piece

    turned = turn_taps(f_ref)

    def tile_at(index):
        return t_ref[index] if index < EARLY else late[index - EARLY]

    for d in range(nb):
        for k in (2 * d, 2 * d + 1):
            if k + 1 >= EARLY:
                late[k + 1 - EARLY] = toeplitz_tile(turned, k)
        span = -(-(nb - d) * width // BLK) * BLK
        moved = gb[d * width : d * width + span, :]
        mid = tile_at(2 * d + 1)
        up = tile_at(2 * d + 2)
        down = tile_at(2 * d)
        tile = jnp.concatenate(
            [
                jnp.concatenate([mid, down], axis=1),
                jnp.concatenate([up, mid], axis=1),
            ],
            axis=0,
        )
        if d == 0:
            acc[...] = mm(moved, tile)
        else:
            acc[:span, :] += mm(moved, tile)
        prod = mm(x_ref[:, :span], moved)
        put(2 * d, prod[:TILE, :TILE], fresh=d == 0)
        put(2 * d + 1, prod[:TILE, TILE:] + prod[TILE:, :TILE], fresh=True)
        put(2 * d + 2, prod[TILE:, TILE:], fresh=True)

    for s in range(senders):
        for k in range(8):
            a = (s * 4 + k // 2) * width
            lo = k % 2 * TILE
            o_ref[s, k * width : (k + 1) * width, :] = acc[
                a : a + width, lo : lo + TILE
            ].astype(BF16)

    lane = iota((PART, TILE), 1)
    turned = lane <= iota((PART, TILE), 0)
    spill = jnp.zeros((PART, TILE), F32)
    carry = jnp.zeros((1, TILE), F32)
    lines = []
    for k in range(2 * nb + 2):
        total = spill
        if k <= 2 * nb:
            low = corr[0, k * PART : (k + 1) * PART, :]
            spill = jnp.zeros((PART, TILE), F32)
            for part in range(1, TILE // PART):
                by = part * PART
                move = pltpu.roll(corr[part, k * PART : (k + 1) * PART, :], by, 1)
                low = low + jnp.where(lane >= by, move, 0.0)
                spill = spill + jnp.where(lane < by, move, 0.0)
            total = total + low
        move = pltpu.roll(total, 1, 1, stride=1, stride_axis=0)
        line = jnp.sum(jnp.where(turned, 0.0, move), axis=0, keepdims=True)
        if k >= 2:
            lines.append(line + carry)
        carry = jnp.sum(jnp.where(turned, move, 0.0), axis=0, keepdims=True)

    at = 8 * width
    for s in range(senders):
        full = jnp.concatenate(lines[s * TAIL : (s + 1) * TAIL], axis=0)
        first = full.astype(BF16)
        rest = full - first.astype(F32)
        second = rest.astype(BF16)
        third = (rest - second.astype(F32)).astype(BF16)
        o_ref[s, at : at + 2 * TAIL, :] = jnp.concatenate([first, second], axis=0)
        o_ref[s, at + 2 * TAIL :, :] = third


def convolve(spot, g, xt, tiles, taps):
    senders = g.shape[0] // 2
    width = g.shape[1]
    nb = 4 * senders
    top = nb * width
    return pl.pallas_call(
        conv_body,
        out_shape=jax.ShapeDtypeStruct((senders, 8 * width + 3 * TAIL, TILE), BF16),
        in_specs=[pl.BlockSpec(memory_space=pltpu.SMEM)]
        + [pl.BlockSpec(memory_space=pltpu.VMEM)] * 4,
        scratch_shapes=[
            pltpu.VMEM((top + BLK, BLK), BF16),
            pltpu.VMEM((top, BLK), F32),
            pltpu.VMEM((TILE // PART, (2 * nb + 1) * PART, TILE), F32),
            pltpu.VMEM((2 * nb + 1 - EARLY, TILE, TILE), BF16),
        ],
        name="convolve",
        compiler_params=pltpu.CompilerParams(vmem_limit_bytes=VMEM_MIB * 2**20),
        cost_estimate=cost(6 * 10**9, 4 * 10**6),
    )(spot, g, xt, tiles, taps)


def finish_body(m_ref, o_ref, f_ref):
    groups, rows, _ = m_ref.shape
    width = (rows - 3 * TAIL) // 8
    for k in range(8):
        at = slice(k * width, (k + 1) * width)
        for h in range(groups // 4):
            four = [m_ref[4 * h + i, at, :].astype(F32) for i in range(4)]
            flat = jnp.concatenate(four, axis=0)
            o_ref[k * TILE : (k + 1) * TILE, h * TILE : (h + 1) * TILE] = flat.T.astype(BF16)
    at = 8 * width
    for g in range(groups):
        both = m_ref[g, at : at + 2 * TAIL, :].astype(F32)
        total = both[:TAIL] + both[TAIL:] + m_ref[g, at + 2 * TAIL :, :].astype(F32)
        for j in range(TAIL):
            f_ref[g : g + 1, j * TILE : (j + 1) * TILE] = total[j : j + 1, :]


def finish(major):
    groups, rows, lanes = major.shape
    width = (rows - 3 * TAIL) // 8
    return pl.pallas_call(
        finish_body,
        out_shape=(
            jax.ShapeDtypeStruct((8 * lanes, groups * width), BF16),
            jax.ShapeDtypeStruct((groups, TAIL * lanes), F32),
        ),
        name="finish",
        compiler_params=params(),
        cost_estimate=cost(10**6, 4 * major.size),
    )(major)


def on_device(conv_input, grad_out, out_weight, filters):
    groups = filters.shape[0]
    width = conv_input.shape[1] // groups
    seq = ("y", "zlo")
    near = ("zlo", "zhi")
    x = lax.axis_index("x").astype(jnp.int32)
    core = lax.axis_index("core").astype(jnp.int32)
    zhi = lax.axis_index("zhi").astype(jnp.int32)
    half = grad_out.shape[0] // 2
    spots = jnp.stack([x, core, zhi])
    spots, grad_out = lax.optimization_barrier((spots, grad_out))
    before = lax.ppermute(grad_out, "x", X_UP)
    after = lax.ppermute(grad_out, "x", X_DOWN)
    near_own = lax.ppermute(grad_out, near, Z_NEAR)
    other_weight = lax.ppermute(out_weight, "core", SWAP)
    far_a = lax.ppermute(before[:half], "x", X_UP)
    far_b = lax.ppermute(after[half:], "x", X_DOWN)
    turned = prep_input(conv_input, groups, width)
    turned = lax.all_to_all(turned, seq, 0, 0, tiled=True)
    near_before = lax.ppermute(near_own, "x", X_UP)
    near_after = lax.ppermute(near_own, "x", X_DOWN)
    near_far_a = lax.ppermute(far_a, near, Z_NEAR)
    near_far_b = lax.ppermute(far_b, near, Z_NEAR)
    taps = lax.dynamic_index_in_dim(filters, lax.axis_index(seq), 0, False)
    taps = taps.reshape(-1, TILE)
    tiles, xt = ready(taps, turned)
    shifts = [(0, 0), (3, 0), (1, 0), (2, 0), (2, half)]
    g, near_own = project(
        spots, out_weight, other_weight,
        [grad_out, before, after, far_a, far_b], shifts, later=near_own,
    )
    g = project(
        spots, out_weight, other_weight,
        [near_own, near_before, near_after, near_far_a, near_far_b], shifts, g=g,
    )
    g = g.reshape(2 * groups, width, -1)
    g = lax.all_to_all(g, ("core",) + seq, 0, 0, tiled=True)
    major = convolve(spots, g, xt, tiles, taps)
    major = lax.all_to_all(major, seq, 0, 0, tiled=True)
    return finish(major)


def solution(mesh):
    fine = Mesh(
        mesh.devices.reshape(4, 2, 2, 4, 2),
        ("y", "zlo", "zhi", "x", "core"),
        axis_types=(jax.sharding.AxisType.Auto,) * 5,
    )
    seq = ("y", "zlo")
    chan = ("zhi", "x", "core")
    in_specs = (P(seq, chan), P(seq + chan, None), P(chan, None), P(chan, None))
    out_specs = (P(seq, chan), P(chan, seq))
    return jax.shard_map(
        on_device, mesh=fine, in_specs=in_specs, out_specs=out_specs, check_vma=False
    )
```
